32 devices in a mesh: rep: 8 (over z, core), zero: 4 (over y, x).
Axes of the slice: x: 2, y: 2, z: 4, core: 2. Of those that a mesh axis runs over, the one named last changes fastest.
Arguments:
- tokens: bfloat16 [32768, 1024], P(('rep', 'zero')), may hold values from -6 to 6
- segment_ids: int32 [32768], P(('rep', 'zero')), may hold values from 0 to 63, never falling along the last dimension, each value on 1 to 2048 neighbouring positions
- cotangent: bfloat16 [32768, 1024], P(('rep', 'zero')), may hold values from -6 to 6
- lead_gain: float32 [1024], P('zero'), may hold values from 0.25 to 1.75
- inner_weight: float32 [1024, 4384], P('zero'), may hold values from -0.1875 to 0.1875
- conv_table: float32 [5, 2304], P(None, 'zero'), may hold values from -3 to 3
- head_table: float32 [3, 32], P(None, 'zero'), may hold values from -6 to 2, as said below
- gate_gain: float32 [2048], P('zero'), may hold values from 0.25 to 1.75
- outer_weight: float32 [2048, 1024], P('zero'), may hold values from -0.125 to 0.125
- lead_first: float32 [1024], P('zero'), may hold values from -6 to 6
- inner_first: float32 [1024, 4384], P('zero'), may hold values from -6 to 6
- conv_first: float32 [5, 2304], P(None, 'zero'), may hold values from -6 to 6
- head_first: float32 [3, 32], P(None, 'zero'), may hold values from -6 to 6
- gate_first: float32 [2048], P('zero'), may hold values from -6 to 6
- outer_first: float32 [2048, 1024], P('zero'), may hold values from -6 to 6
- lead_second: float32 [1024], P('zero'), may hold values from 1 to 100
- inner_second: float32 [1024, 4384], P('zero'), may hold values from 1 to 100
- conv_second: float32 [5, 2304], P(None, 'zero'), may hold values from 1 to 100
- head_second: float32 [3, 32], P(None, 'zero'), may hold values from 1 to 100
- gate_second: float32 [2048], P('zero'), may hold values from 1 to 100
- outer_second: float32 [2048, 1024], P('zero'), may hold values from 1 to 100
Outputs:
- mixed: bfloat16 [32768, 1024], P(('rep', 'zero'))
- tokens_grad: bfloat16 [32768, 1024], P(('rep', 'zero'))
- lead_grad: float32 [1024], P('zero')
- inner_grad: float32 [1024, 4384], P('zero')
- conv_grad: float32 [5, 2304], P(None, 'zero')
- head_grad: float32 [3, 32], P(None, 'zero')
- gate_grad: float32 [2048], P('zero')
- outer_grad: float32 [2048, 1024], P('zero')
- lead_fresh: float32 [1024], P('zero')
- inner_fresh: float32 [1024, 4384], P('zero')
- conv_fresh: float32 [5, 2304], P(None, 'zero')
- head_fresh: float32 [3, 32], P(None, 'zero')
- gate_fresh: float32 [2048], P('zero')
- outer_fresh: float32 [2048, 1024], P('zero')
- first_lead: float32 [1024], P('zero')
- first_inner: float32 [1024, 4384], P('zero')
- first_conv: float32 [5, 2304], P(None, 'zero')
- first_head: float32 [3, 32], P(None, 'zero')
- first_gate: float32 [2048], P('zero')
- first_outer: float32 [2048, 1024], P('zero')
- second_lead: float32 [1024], P('zero')
- second_inner: float32 [1024, 4384], P('zero')
- second_conv: float32 [5, 2304], P(None, 'zero')
- second_head: float32 [3, 32], P(None, 'zero')
- second_gate: float32 [2048], P('zero')
- second_outer: float32 [2048, 1024], P('zero')
The draws below stay inside these ranges and needn't reach their ends.
Inputs may be any that keep to these rules, and one draw needn't show every extreme that they name: `segment_ids`: document numbers never fall along the tokens; a sequence begins a new scan and convolution at its first token even if its document continued in the previous sequence. `head_table`: row 0 lies in -6 to -2, row 1 in 0 to 2, row 2 in 1 to 2.
All inputs are finite; a program needn't handle non-finite values.
Results may differ from the reference program's by a relative error of at most 0.025.
Values may be sent and summed in bfloat16 or wider, within the bound.
No kernel may reach another device: no remote copies, remote signals or barrier semaphores. Data moves between devices by JAX's collectives and lax.ppermute only.
A program may use at most 256 MiB of HBM per device.

```python
import math
import jax
import jax.numpy as jnp
import numpy as np
from jax import lax

D = 1024
DI = 2048
H = 32
P_SIZE = 64
N = 128
K = 4
LEN = 1024
CONV = 2304
PROJ = 4384
TOKENS = 32768
DOCS = 64


def draw_head_table(key, part):
    bias_row = jax.random.uniform(jax.random.fold_in(key, 11), (H,), jnp.float32, -6.0, -2.0)
    decay_row = jax.random.uniform(jax.random.fold_in(key, 12), (H,), jnp.float32, 0.0, 2.0)
    skip_row = jax.random.uniform(jax.random.fold_in(key, 13), (H,), jnp.float32, 1.0, 2.0)
    return jnp.stack([bias_row, decay_row, skip_row])


def block_scale(key, dims, cuts, least, top_value):
    factor_of, own = 1.0, jax.random.fold_in(key, 6)
    for axis_at, shards_of in cuts:
        steps = jnp.exp(jax.random.uniform(jax.random.fold_in(own, axis_at), (shards_of,), jnp.float32, least / len(cuts), top_value / len(cuts)))
        factor_of = factor_of * jnp.repeat(steps, dims[axis_at] // shards_of).reshape([-1 if axis == axis_at else 1 for axis in range(len(dims))])
    return factor_of


def length_profile(count, total, bound, lean):
    portions = [(1 << 20) // math.isqrt(grade ** lean) + 1 for grade in range(2, count + 1)]
    spare, holding = total - bound - (count - 1), [1] * (count - 1)
    while spare > 0:
        free = [i for i in range(count - 1) if holding[i] < bound]
        mass, remaining = sum([portions[i] for i in free]), spare
        for i in free:
            addition = min(bound - holding[i], max(1, remaining * portions[i] // mass), spare)
            holding[i] = holding[i] + addition
            spare = spare - addition
    return np.array([bound] + holding)


def uneven(own_key, amount, total, bound, lean):
    if amount == 2:
        one = jax.random.randint(own_key, (), max(1, total - bound), min(bound, total - 1) + 1)
        return jnp.stack([one, total - one])
    lengths = jnp.asarray(length_profile(amount, total, bound, lean), jnp.int32)
    twos = (amount - 1) // 2
    source_of, sink = lengths[1:1 + 2 * twos:2], lengths[2:2 + 2 * twos:2]
    room = jnp.minimum(source_of - 1, bound - sink)
    moved = jax.random.randint(jax.random.fold_in(own_key, 1), (twos,), 0, 1 << 20) % (room + 1)
    lengths = lengths.at[1:1 + 2 * twos:2].set(source_of - moved).at[2:2 + 2 * twos:2].set(sink + moved)
    return lengths[jax.random.permutation(jax.random.fold_in(own_key, 2), amount)]


def bell_draw(rng, dims, scale, reach, cuts=(), dtype=jnp.bfloat16):
    drawn = scale * jax.random.normal(rng, dims, jnp.float32)
    if cuts:
        drawn = drawn * block_scale(rng, dims, cuts, -0.22, 0.18)
    return jnp.clip(drawn, -reach, reach).astype(dtype)


def setup_inputs(seed: int = 0) -> dict:
    streams_of = jax.random.split(jax.random.key(seed), 22)
    tokens = bell_draw(streams_of[0], (TOKENS, D), 1.0, 6.0, ((0, 32),))
    segment_ids = jnp.searchsorted(jnp.cumsum(uneven(streams_of[1], DOCS, TOKENS, 2 * LEN, 1)), jnp.arange(TOKENS), side="right").astype(jnp.int32)
    cotangent = bell_draw(streams_of[2], (TOKENS, D), 1.0, 6.0, ((0, 32),))
    lead_gain = jnp.clip(1.0 + 0.15 * jax.random.normal(streams_of[3], (D,), jnp.float32), 0.25, 1.75)
    inner_weight = bell_draw(streams_of[4], (D, PROJ), D ** -0.5, 0.1875, ((0, 4),), jnp.float32)
    conv_table = bell_draw(streams_of[5], (K + 1, CONV), K ** -0.5, 3.0, ((1, 4),), jnp.float32)
    head_table = draw_head_table(jax.random.fold_in(streams_of[21], 71), 0)
    gate_gain = jnp.clip(1.0 + 0.15 * jax.random.normal(streams_of[7], (DI,), jnp.float32), 0.25, 1.75)
    outer_weight = bell_draw(streams_of[8], (DI, D), DI ** -0.5, 0.125, ((0, 4),), jnp.float32)
    lead_first = bell_draw(streams_of[9], (D,), 1.0, 6.0, ((0, 4),), jnp.float32)
    inner_first = bell_draw(streams_of[10], (D, PROJ), 1.0, 6.0, ((0, 4),), jnp.float32)
    conv_first = bell_draw(streams_of[11], (K + 1, CONV), 1.0, 6.0, ((1, 4),), jnp.float32)
    head_first = bell_draw(streams_of[12], (3, H), 1.0, 6.0, ((1, 4),), jnp.float32)
    gate_first = bell_draw(streams_of[13], (DI,), 1.0, 6.0, ((0, 4),), jnp.float32)
    outer_first = bell_draw(streams_of[14], (DI, D), 1.0, 6.0, ((0, 4),), jnp.float32)
    lead_second = jnp.clip(jnp.exp(math.log(100.0) - 4.6051702 * jax.random.uniform(streams_of[15], (D,), jnp.float32) ** block_scale(streams_of[15], (D,), ((0, 4),), -0.2, 0.2)), 1.0, 100.0)
    inner_second = jnp.clip(jnp.exp(math.log(100.0) - 4.6051702 * jax.random.uniform(streams_of[16], (D, PROJ), jnp.float32) ** block_scale(streams_of[16], (D, PROJ), ((0, 4),), -0.2, 0.2)), 1.0, 100.0)
    conv_second = jnp.clip(jnp.exp(math.log(100.0) - 4.6051702 * jax.random.uniform(streams_of[17], (K + 1, CONV), jnp.float32) ** block_scale(streams_of[17], (K + 1, CONV), ((1, 4),), -0.2, 0.2)), 1.0, 100.0)
    head_second = jnp.clip(jnp.exp(math.log(100.0) - 4.6051702 * jax.random.uniform(streams_of[18], (3, H), jnp.float32) ** block_scale(streams_of[18], (3, H), ((1, 4),), -0.2, 0.2)), 1.0, 100.0)
    gate_second = jnp.clip(jnp.exp(math.log(100.0) - 4.6051702 * jax.random.uniform(streams_of[19], (DI,), jnp.float32) ** block_scale(streams_of[19], (DI,), ((0, 4),), -0.2, 0.2)), 1.0, 100.0)
    outer_second = jnp.clip(jnp.exp(math.log(100.0) - 4.6051702 * jax.random.uniform(streams_of[20], (DI, D), jnp.float32) ** block_scale(streams_of[20], (DI, D), ((0, 4),), -0.2, 0.2)), 1.0, 100.0)
    return {"tokens": tokens, "segment_ids": segment_ids, "cotangent": cotangent, "lead_gain": lead_gain, "inner_weight": inner_weight, "conv_table": conv_table, "head_table": head_table, "gate_gain": gate_gain, "outer_weight": outer_weight, "lead_first": lead_first, "inner_first": inner_first, "conv_first": conv_first, "head_first": head_first, "gate_first": gate_first, "outer_first": outer_first, "lead_second": lead_second, "inner_second": inner_second, "conv_second": conv_second, "head_second": head_second, "gate_second": gate_second, "outer_second": outer_second}


@jax.custom_vjp
def low(v):
    return lax.optimization_barrier(v.astype(jnp.bfloat16)).astype(jnp.float32)

@jax.custom_vjp
def low_back(v):
    return v

def low_keep(v):
    return (low(v), None)

def low_pass(kept, grad):
    return (grad,)

def back_keep(v):
    return (v, None)

def back_low(kept, grad):
    return (low(grad),)
low.defvjp(low_keep, low_pass)
low_back.defvjp(back_keep, back_low)
norm_eps = 1e-05
beta_one = 0.9
beta_two = 0.95
learn_rate = 0.01
decay_rate = 0.1
adam_eps = 1e-08
adam_step = 3
highest = lax.Precision.HIGHEST

def convolve(conv_in, kernel, doc_ids):
    summed = kernel[K] + conv_in * kernel[K - 1]
    for step_back in range(1, K):
        shifted = jnp.concatenate([jnp.zeros((step_back, conv_in.shape[1]), jnp.float32), conv_in[:-step_back]], axis=0)
        before = jnp.concatenate([jnp.full((step_back,), -1, jnp.int32), doc_ids[:-step_back]])
        summed = summed + jnp.where((before == doc_ids)[:, None], shifted, 0.0) * kernel[K - 1 - step_back]
    return summed

def quadratic(values, entry_b, entry_c, steps, rates, doc_ids):
    length = values.shape[0]
    log_decay = jnp.cumsum(steps * rates, axis=0)
    causal = lax.broadcasted_iota(jnp.int32, (length, length), 0) >= lax.broadcasted_iota(jnp.int32, (length, length), 1)
    linked = causal & (doc_ids[:, None] == doc_ids[None, :])
    spread = log_decay.T[:, :, None] - log_decay.T[:, None, :]
    decays = jnp.where(linked, jnp.exp(jnp.where(linked, spread, 0.0)), 0.0)
    scores = jnp.dot(entry_c, entry_b.T, precision=highest)
    weights = decays * scores * steps.T[:, None, :]
    return jnp.einsum('hts,shp->thp', weights, values, precision=highest)

def sequence_pass(used, inputs, doc_ids):
    lead_gain, inner_weight, conv_table, head_table, gate_gain, outer_weight = used
    normed = low(inputs * lax.rsqrt(lax.optimization_barrier(jnp.mean(inputs * inputs, axis=-1, keepdims=True)) + norm_eps) * lead_gain)
    projected = low_back(jnp.dot(normed, inner_weight, precision=highest))
    gate_in = projected[:, :DI]
    conv_in = projected[:, DI:DI + CONV]
    step_in = projected[:, DI + CONV:]
    acts = low(jax.nn.silu(convolve(conv_in, conv_table, doc_ids)))
    steps = jax.nn.softplus(step_in + head_table[0])
    rates = -jnp.exp(head_table[1])
    values = acts[:, :DI].reshape(-1, H, P_SIZE)
    mixed_y = quadratic(values, acts[:, DI:DI + N], acts[:, DI + N:], steps, rates, doc_ids)
    mixed_y = mixed_y + head_table[2][None, :, None] * values
    gated = mixed_y.reshape(-1, DI) * jax.nn.silu(gate_in)
    gnormed = low(gated * lax.rsqrt(lax.optimization_barrier(jnp.mean(gated * gated, axis=-1, keepdims=True)) + norm_eps) * gate_gain)
    return inputs + jnp.dot(gnormed, outer_weight, precision=highest)

def adam(weight, grad, first, second):
    first_new = beta_one * first + (1.0 - beta_one) * grad
    second_new = beta_two * second + (1.0 - beta_two) * grad * grad
    first_hat = first_new / (1.0 - beta_one ** adam_step)
    second_hat = second_new / (1.0 - beta_two ** adam_step)
    fresh = weight - learn_rate * (first_hat / (jnp.sqrt(second_hat) + adam_eps) + decay_rate * weight)
    return (fresh, first_new, second_new)

def reference(tokens, segment_ids, cotangent, lead_gain, inner_weight, conv_table, head_table, gate_gain, outer_weight, lead_first, inner_first, conv_first, head_first, gate_first, outer_first, lead_second, inner_second, conv_second, head_second, gate_second, outer_second):
    masters = (lead_gain, inner_weight, conv_table, head_table, gate_gain, outer_weight)
    sequences = TOKENS // LEN
    inputs = tokens.astype(jnp.float32).reshape(sequences, LEN, D)
    doc_ids = segment_ids.reshape(sequences, LEN)

    def forward(weights, batch):
        used = tuple((low(weight) for weight in weights))

        def one_step(carry, item):
            return (carry, sequence_pass(used, item[0], item[1]))
        carry_out, outputs = lax.scan(jax.checkpoint(one_step), jnp.zeros((), jnp.float32), (batch, doc_ids))
        return outputs
    outputs, pullback = jax.vjp(forward, masters, inputs)
    weight_grads, input_grads = pullback(cotangent.astype(jnp.float32).reshape(sequences, LEN, D))
    lead_up = adam(lead_gain, weight_grads[0], lead_first, lead_second)
    inner_up = adam(inner_weight, weight_grads[1], inner_first, inner_second)
    conv_up = adam(conv_table, weight_grads[2], conv_first, conv_second)
    head_up = adam(head_table, weight_grads[3], head_first, head_second)
    gate_up = adam(gate_gain, weight_grads[4], gate_first, gate_second)
    outer_up = adam(outer_weight, weight_grads[5], outer_first, outer_second)
    return (outputs.reshape(TOKENS, D).astype(jnp.bfloat16), input_grads.reshape(TOKENS, D).astype(jnp.bfloat16), weight_grads[0], weight_grads[1], weight_grads[2], weight_grads[3], weight_grads[4], weight_grads[5], lead_up[0], inner_up[0], conv_up[0], head_up[0], gate_up[0], outer_up[0], lead_up[1], inner_up[1], conv_up[1], head_up[1], gate_up[1], outer_up[1], lead_up[2], inner_up[2], conv_up[2], head_up[2], gate_up[2], outer_up[2])
```

```python
import jax
import jax.numpy as jnp
from jax import lax
from jax.experimental import pallas as pl
from jax.experimental.pallas import tpu as pltpu
from jax.sharding import PartitionSpec as P

DI = 2048
H = 32
N = 128
K = 4
Q = 128
LEN = 1024
CONV = 2304
WIDE = CONV + H
CH = LEN // Q
PAIRS = H // 2
norm_eps = 1e-05
LOG2E = 1.4426950408889634
NEG = -1e30
f32 = jnp.float32
bf16 = jnp.bfloat16
highest = lax.Precision.HIGHEST


def sigmoid(v):
    return 0.5 * jnp.tanh(0.5 * v) + 0.5


def dot(a, b):
    return jnp.dot(a, b, preferred_element_type=f32)


def dot_nt(a, b):
    return lax.dot_general(a, b, (((1,), (1,)), ((), ())), preferred_element_type=f32)


def lanes(col, width=128):
    return jnp.broadcast_to(col, (col.shape[0], width))


def iota(shape, dim):
    return lax.broadcasted_iota(jnp.int32, shape, dim)


def softplus(v):
    u = jnp.exp(-jnp.abs(v))
    series = u * (1.0 - u * (0.5 - u * (1.0 / 3.0 - u * 0.25)))
    return jnp.maximum(v, 0.0) + jnp.where(u < 0.01, series, jnp.log(1.0 + u))


def decay_terms(step, head):
    pre = step + head[0:1, :]
    dt = softplus(pre)
    lower = (iota((Q, Q), 0) >= iota((Q, Q), 1)).astype(f32)
    a = jnp.dot(lower, dt * head[1:2, :], precision=highest, preferred_element_type=f32) * LOG2E
    b = a - jnp.log(dt) * LOG2E
    return pre, dt, a, b


def fwd_kernel(ids_s, cin, step, rows, taps, head, dskip, y_out, act_out, ds_out, st_out, state, xs, cs, xe, keep):
    c = pl.program_id(0)

    @pl.when(c == 0)
    def _():
        state[...] = jnp.zeros_like(state)
        xs[0:8, :] = jnp.zeros((8, CONV), f32)

    turned = rows[0].T
    m1 = lanes(turned[:, 1:2])
    m2 = lanes(turned[:, 2:3])
    m3 = lanes(turned[:, 3:4])

    def conv_tile(i, _):
        at = pl.ds(pl.multiple_of(i * 128, 128), 128)
        xs[8:136, at] = cin[:, at].astype(f32)
        x0 = xs[8:136, at]
        out = taps[4:5, at] + x0 * taps[3:4, at]
        out += xs[7:135, at] * m1 * taps[2:3, at]
        out += xs[6:134, at] * m2 * taps[1:2, at]
        out += xs[5:133, at] * m3 * taps[0:1, at]
        sig = sigmoid(out)
        act = out * sig
        act_out[:, at] = act.astype(bf16)
        ds_out[:, at] = (sig + act * (1.0 - sig)).astype(bf16)
        return 0

    lax.fori_loop(0, CONV // 128, conv_tile, 0)
    xs[0:8, :] = xs[128:136, :]

    pre, dt, a, b = decay_terms(step[...], head)
    a_t = a.T
    b_t = b.T
    bb = act_out[:, DI : DI + N]
    cc = act_out[:, DI + N :]
    g = dot_nt(cc, bb)
    row_id = lanes(turned[:, 0:1])
    linked = (iota((Q, Q), 0) >= iota((Q, Q), 1)) & (row_id == rows[0, 0:1, :])
    bias = jnp.where(linked, 0.0, NEG)
    prev = jnp.where(c == 0, -1, ids_s[jnp.maximum(c * Q - 1, 0)])
    last = ids_s[c * Q + Q - 1]
    carried = jnp.where(row_id == prev.astype(f32), 0.0, NEG)
    ending = jnp.where(row_id == last.astype(f32), 0.0, NEG)
    kept = jnp.where(last == prev, 0.0, NEG)
    s_low = state[...].astype(bf16)
    st_out[0] = s_low
    cs[...] = dot(cc, s_low)
    left = iota((Q, 128), 1) < 64
    for p in range(PAIRS):
        at = slice(p * 128, p * 128 + 128)
        a0 = lanes(a[:, 2 * p : 2 * p + 1])
        a1 = lanes(a[:, 2 * p + 1 : 2 * p + 2])
        w0 = jnp.exp2(a0 - b_t[2 * p : 2 * p + 1, :] + bias) * g
        w1 = jnp.exp2(a1 - b_t[2 * p + 1 : 2 * p + 2, :] + bias) * g
        w = jnp.concatenate([w0, w1], axis=1).astype(bf16)
        xp = act_out[:, at]
        zero = jnp.zeros_like(xp)
        xx = jnp.concatenate([jnp.where(left, xp, zero), jnp.where(left, zero, xp)], axis=0)
        y = dot(w, xx)
        ap = jnp.where(left, a0, a1)
        y += jnp.exp2(ap + carried) * cs[:, at]
        xf = xp.astype(f32)
        y_out[:, at] = y + dskip[0:1, at] * xf
        bp = jnp.where(left, lanes(b[:, 2 * p : 2 * p + 1]), lanes(b[:, 2 * p + 1 : 2 * p + 2]))
        a_end = ap[Q - 1 : Q, :]
        xe[:, at] = (jnp.exp2(a_end - bp + ending) * xf).astype(bf16)
        keep[0:1, at] = jnp.exp2(a_end + kept)
    b_turn = bb.astype(f32).T.astype(bf16)
    state[...] = state[...] * keep[0:1, :] + dot(b_turn, xe[...])


def full_spec(shape):
    return pl.BlockSpec(shape, lambda i, *_: (0,) * len(shape))


def scan_forward(ids, rows, conv_in, step_in, taps, head, dskip):
    return pl.pallas_call(
        fwd_kernel,
        grid_spec=pltpu.PrefetchScalarGridSpec(
            num_scalar_prefetch=1,
            grid=(CH,),
            in_specs=[
                pl.BlockSpec((Q, CONV), lambda i, *_: (i, 0)),
                pl.BlockSpec((Q, 128), lambda i, *_: (i, 0)),
                pl.BlockSpec((1, 8, Q), lambda i, *_: (i, 0, 0)),
                full_spec((8, CONV)),
                full_spec((8, 128)),
                full_spec((8, DI)),
            ],
            out_specs=[
                pl.BlockSpec((Q, DI), lambda i, *_: (i, 0)),
                pl.BlockSpec((Q, CONV), lambda i, *_: (i, 0)),
                pl.BlockSpec((Q, CONV), lambda i, *_: (i, 0)),
                pl.BlockSpec((1, N, DI), lambda i, *_: (i, 0, 0)),
            ],
            scratch_shapes=[
                pltpu.VMEM((N, DI), f32),
                pltpu.VMEM((Q + 8, CONV), f32),
                pltpu.VMEM((Q, DI), f32),
                pltpu.VMEM((Q, DI), bf16),
                pltpu.VMEM((8, DI), f32),
            ],
        ),
        out_shape=[
            jax.ShapeDtypeStruct((LEN, DI), f32),
            jax.ShapeDtypeStruct((LEN, CONV), bf16),
            jax.ShapeDtypeStruct((LEN, CONV), bf16),
            jax.ShapeDtypeStruct((CH, N, DI), bf16),
        ],
        name="scan_forward",
    )(ids, conv_in, step_in, rows, taps, head, dskip)


def bwd_kernel(ids_s, act, ds, cin, step, rows, taps, head, dskip, st, yg, y, gx_out, gconv, ghead, gskip, adj, cg, bz, xe, ye, keep, after, pick):
    i = pl.program_id(0)
    c = CH - 1 - i

    @pl.when(i == 0)
    def _():
        adj[...] = jnp.zeros_like(adj)
        cg[Q : Q + 8, :] = jnp.zeros((8, CONV), f32)
        after[...] = jnp.zeros_like(after)
        gconv[...] = jnp.zeros_like(gconv)
        ghead[...] = jnp.zeros_like(ghead)
        gskip[...] = jnp.zeros_like(gskip)
        pick[...] = jnp.where((iota((DI, 128), 0) >> 6) == iota((DI, 128), 1), 1.0, 0.0).astype(bf16)

    pre, dt, a, b = decay_terms(step[...], head)
    a_t = a.T
    bb = act[:, DI : DI + N]
    cc = act[:, DI + N :]
    g = dot_nt(bb, cc)
    turned = rows[0].T
    row_id = lanes(turned[:, 0:1])
    linked = (iota((Q, Q), 0) <= iota((Q, Q), 1)) & (row_id == rows[0, 0:1, :])
    bias = jnp.where(linked, 0.0, NEG)
    prev = jnp.where(c == 0, -1, ids_s[jnp.maximum(c * Q - 1, 0)])
    last = ids_s[c * Q + Q - 1]
    carried = jnp.where(row_id == prev.astype(f32), 0.0, NEG)
    ending = jnp.where(row_id == last.astype(f32), 0.0, NEG)
    kept = jnp.where(last == prev, 0.0, NEG)
    z_low = adj[...].astype(bf16)
    bz[...] = dot(bb, z_low)
    left = iota((Q, 128), 1) < 64
    g_grad = jnp.zeros((Q, Q), f32)
    dl = jnp.zeros((Q, 128), f32)
    own = jnp.zeros((Q, 128), f32)
    for p in range(PAIRS):
        at = slice(p * 128, p * 128 + 128)
        b0 = lanes(b[:, 2 * p : 2 * p + 1])
        b1 = lanes(b[:, 2 * p + 1 : 2 * p + 2])
        w0 = jnp.exp2(a_t[2 * p : 2 * p + 1, :] - b0 + bias)
        w1 = jnp.exp2(a_t[2 * p + 1 : 2 * p + 2, :] - b1 + bias)
        xp = act[:, at]
        yp = yg[:, at]
        zero = jnp.zeros_like(yp)
        yy = jnp.concatenate([jnp.where(left, yp, zero), jnp.where(left, zero, yp)], axis=0)
        m = dot_nt(xp, yy)
        g_grad += w0 * m[:, :Q] + w1 * m[:, Q:]
        w = jnp.concatenate([w0 * g, w1 * g], axis=1).astype(bf16)
        v = dot(w, yy)
        bp = jnp.where(left, b0, b1)
        ap = jnp.where(left, lanes(a[:, 2 * p : 2 * p + 1]), lanes(a[:, 2 * p + 1 : 2 * p + 2]))
        a_end = ap[Q - 1 : Q, :]
        fade = jnp.exp2(a_end - bp + ending)
        v += fade * bz[:, at]
        xf = xp.astype(f32)
        yf = yp.astype(f32)
        xg = v + dskip[0:1, at] * yf
        cg[0:Q, at] = xg
        r = yf * y[:, at] - xf * xg
        r_hi = r.astype(bf16)
        r_lo = (r - r_hi.astype(f32)).astype(bf16)
        e = pick[at, :]
        dl += dot(jnp.concatenate([r_hi, r_lo], axis=1), jnp.concatenate([e, e], axis=0))
        own += dot((xf * v).astype(bf16), e)
        xe[:, at] = (fade * xf).astype(bf16)
        ye[:, at] = (jnp.exp2(ap + carried) * yf).astype(bf16)
        keep[0:1, at] = jnp.exp2(a_end + kept)
        gskip[0:1, at] += jnp.sum(xf * yf, axis=0, keepdims=True)
    cg[0:Q, DI : DI + N] = dot(g_grad.astype(bf16), cc) + dot_nt(xe[...], z_low)
    cg[0:Q, DI + N :] = dot(g_grad.T.astype(bf16), bb) + dot_nt(ye[...], st[0])
    c_turn = cc.astype(f32).T.astype(bf16)
    adj_in = adj[...] * keep[0:1, :] + dot(c_turn, ye[...])
    adj[...] = adj_in

    upper = (iota((Q, Q), 0) <= iota((Q, Q), 1)).astype(f32)
    a_grad = jnp.dot(upper, dl, precision=highest, preferred_element_type=f32) + after[0:1, :]
    flux = jnp.sum(adj_in * st[0].astype(f32), axis=0, keepdims=True)
    flux_hi = flux.astype(bf16)
    flux_lo = (flux - flux_hi.astype(f32)).astype(bf16)
    both = dot(jnp.concatenate([flux_hi, flux_lo], axis=0), pick[...])
    after[0:1, :] = both[0:1, :] + both[1:2, :]
    rate = head[1:2, :]
    sig = 1.0 / (1.0 + jnp.exp(-pre))
    ratio = jnp.where(pre < -15.0, 1.0, sig / dt)
    step_grad = own * ratio + a_grad * rate * sig
    gx_out[:, CONV:] = step_grad[:, :H].astype(bf16)
    ghead[0:1, :] += jnp.sum(step_grad, axis=0, keepdims=True)
    ghead[1:2, :] += jnp.sum(a_grad * dt, axis=0, keepdims=True) * rate

    m1 = lanes(turned[:, 4:5])
    m2 = lanes(turned[:, 5:6])
    m3 = lanes(turned[:, 6:7])

    def conv_tile(j, _):
        at = pl.ds(pl.multiple_of(j * 128, 128), 128)
        s0 = cg[0:Q, at] * ds[:, at].astype(f32)
        cg[0:Q, at] = s0
        s1 = cg[1 : Q + 1, at] * m1
        s2 = cg[2 : Q + 2, at] * m2
        s3 = cg[3 : Q + 3, at] * m3
        gx = s0 * taps[3:4, at] + s1 * taps[2:3, at] + s2 * taps[1:2, at] + s3 * taps[0:1, at]
        gx_out[:, at] = gx.astype(bf16)
        xin = cin[:, at].astype(f32)
        gconv[3:4, at] += jnp.sum(s0 * xin, axis=0, keepdims=True)
        gconv[2:3, at] += jnp.sum(s1 * xin, axis=0, keepdims=True)
        gconv[1:2, at] += jnp.sum(s2 * xin, axis=0, keepdims=True)
        gconv[0:1, at] += jnp.sum(s3 * xin, axis=0, keepdims=True)
        gconv[4:5, at] += jnp.sum(s0, axis=0, keepdims=True)
        return 0

    lax.fori_loop(0, CONV // 128, conv_tile, 0)
    cg[Q : Q + 8, :] = cg[0:8, :]


def scan_backward(ids, rows, acts, dsilu, conv_in, step_in, taps, head, dskip, states, y_grad, y):
    rev = lambda i, *_: (CH - 1 - i, 0)
    rev3 = lambda i, *_: (CH - 1 - i, 0, 0)
    return pl.pallas_call(
        bwd_kernel,
        grid_spec=pltpu.PrefetchScalarGridSpec(
            num_scalar_prefetch=1,
            grid=(CH,),
            in_specs=[
                pl.BlockSpec((Q, CONV), rev),
                pl.BlockSpec((Q, CONV), rev),
                pl.BlockSpec((Q, CONV), rev),
                pl.BlockSpec((Q, 128), rev),
                pl.BlockSpec((1, 8, Q), rev3),
                full_spec((8, CONV)),
                full_spec((8, 128)),
                full_spec((8, DI)),
                pl.BlockSpec((1, N, DI), rev3),
                pl.BlockSpec((Q, DI), rev),
                pl.BlockSpec((Q, DI), rev),
            ],
            out_specs=[
                pl.BlockSpec((Q, WIDE), rev),
                full_spec((8, CONV)),
                full_spec((8, 128)),
                full_spec((8, DI)),
            ],
            scratch_shapes=[
                pltpu.VMEM((N, DI), f32),
                pltpu.VMEM((Q + 8, CONV), f32),
                pltpu.VMEM((Q, DI), f32),
                pltpu.VMEM((Q, DI), bf16),
                pltpu.VMEM((Q, DI), bf16),
                pltpu.VMEM((8, DI), f32),
                pltpu.VMEM((8, 128), f32),
                pltpu.VMEM((DI, 128), bf16),
            ],
        ),
        out_shape=[
            jax.ShapeDtypeStruct((LEN, WIDE), bf16),
            jax.ShapeDtypeStruct((8, CONV), f32),
            jax.ShapeDtypeStruct((8, 128), f32),
            jax.ShapeDtypeStruct((8, DI), f32),
        ],
        name="scan_backward",
    )(ids, acts, dsilu, conv_in, step_in, rows, taps, head, dskip, states, y_grad, y)


GB = 128


def gate_kernel(y, z, gn, gain, low_out, yg_out, zg_out, ggain):
    @pl.when(pl.program_id(0) == 0)
    def _():
        ggain[...] = jnp.zeros_like(ggain)

    zz = z[...].astype(f32)
    yy = y[...]
    sig = sigmoid(zz)
    silu = zz * sig
    gated = yy * silu
    r2 = lax.rsqrt(jnp.sum(gated * gated, axis=-1, keepdims=True) * (1.0 / DI) + norm_eps)
    unit = gated * r2
    k = gain[0:1, :]
    low_out[...] = (unit * k).astype(bf16)
    gnv = gn[...].astype(f32)
    ggain[0:1, :] += jnp.sum(gnv * unit, axis=0, keepdims=True)
    q = gnv * k
    coef = jnp.sum(q * unit, axis=-1, keepdims=True) * (1.0 / DI)
    gg = r2 * (q - unit * coef)
    yg_out[...] = (gg * silu).astype(bf16)
    zg_out[...] = (gg * yy * (sig + silu * (1.0 - sig))).astype(bf16)


def gate(y, z, gn, gain):
    blk = lambda: pl.BlockSpec((GB, DI), lambda i: (i, 0))
    return pl.pallas_call(
        gate_kernel,
        grid=(LEN // GB,),
        in_specs=[blk(), blk(), blk(), pl.BlockSpec((8, DI), lambda i: (0, 0))],
        out_specs=[blk(), blk(), blk(), pl.BlockSpec((8, DI), lambda i: (0, 0))],
        out_shape=[jax.ShapeDtypeStruct((LEN, DI), bf16)] * 3 + [jax.ShapeDtypeStruct((8, DI), f32)],
        name="gate",
    )(y, z, gn, gain)


beta_one = 0.9
beta_two = 0.95
learn_rate = 0.01
decay_rate = 0.1
adam_eps = 1e-08
adam_step = 3


def project_kernel(offs, lhs, *refs, count, half, tile, transposed, tail):
    parts = refs[: 2 * count - 1]
    outs = refs[2 * count - 1 : -3]
    weight, sems, back = refs[-3:]
    out, kept = outs[0], outs[-1]
    j = pl.program_id(0)

    @pl.when(j == 0)
    def _():
        copies = []
        for k, part in enumerate(parts):
            rows = pl.ds(pl.multiple_of(offs[k], half), part.shape[0])
            copies.append(pltpu.make_async_copy(part, weight.at[rows, :], sems.at[k]))
        for copy in copies:
            copy.start()
        for copy in copies:
            copy.wait()
        pltpu.make_async_copy(weight, kept, back.at[0]).start()
        if tail:
            outs[1][:, :tail] = dot(lhs[...], weight[:, weight.shape[1] - tail :])
            outs[1][:, tail:] = jnp.zeros((lhs.shape[0], 128 - tail), f32)

    at = pl.ds(pl.multiple_of(j * tile, tile), tile)
    if transposed:
        out[...] = dot_nt(lhs[...], weight[at, :]).astype(bf16)
    else:
        out[...] = dot(lhs[...], weight[:, at]).astype(bf16)

    @pl.when(j == pl.num_programs(0) - 1)
    def _():
        pltpu.make_async_copy(weight, kept, back.at[0]).wait()


def project(name, offs, lhs, parts, count, transposed=False, tail=0):
    own = parts[0].shape[0]
    rows, cols = own * count, parts[0].shape[1]
    wide = (rows if transposed else cols) - tail
    tile = 256
    outs = [jax.ShapeDtypeStruct((lhs.shape[0], wide), bf16)]
    specs = [pl.BlockSpec((lhs.shape[0], tile), lambda j, *_: (0, j))]
    if tail:
        outs.append(jax.ShapeDtypeStruct((lhs.shape[0], 128), f32))
        specs.append(pl.BlockSpec((lhs.shape[0], 128), lambda j, *_: (0, 0)))
    outs.append(jax.ShapeDtypeStruct((rows, cols), bf16))
    specs.append(pl.BlockSpec(memory_space=pl.ANY))

    def kernel(offs, lhs, *refs):
        project_kernel(offs, lhs, *refs, count=count, half=own // 2, tile=tile, transposed=transposed, tail=tail)

    return pl.pallas_call(
        kernel,
        grid_spec=pltpu.PrefetchScalarGridSpec(
            num_scalar_prefetch=1,
            grid=(wide // tile,),
            in_specs=[pl.BlockSpec(lhs.shape, lambda j, *_: (0, 0))]
            + [pl.BlockSpec(memory_space=pl.ANY)] * len(parts),
            out_specs=specs,
            scratch_shapes=[
                pltpu.VMEM((rows, cols), bf16),
                pltpu.SemaphoreType.DMA((len(parts),)),
                pltpu.SemaphoreType.DMA((1,)),
            ],
        ),
        out_shape=outs,
        name=name,
    )(offs, lhs, *parts)


def tree_sum(items):
    while len(items) > 1:
        items = [items[k] + items[k + 1] for k in range(0, len(items), 2)]
    return items[0]


def adam(weight, grad, first, second):
    first_new = beta_one * first + (1.0 - beta_one) * grad
    second_new = beta_two * second + (1.0 - beta_two) * grad * grad
    first_hat = first_new / (1.0 - beta_one**adam_step)
    second_hat = second_new / (1.0 - beta_two**adam_step)
    fresh = weight - learn_rate * (
        first_hat / (jnp.sqrt(second_hat) + adam_eps) + decay_rate * weight
    )
    return (fresh, first_new, second_new)


def pick_at(array, index, axis=0):
    return lax.dynamic_index_in_dim(array, index, axis, keepdims=False)


def make_body(replicas, owners):
    depth = replicas // 2

    def body(
        tokens,
        segment_ids,
        cotangent,
        lead_gain,
        inner_weight,
        conv_table,
        head_table,
        gate_gain,
        outer_weight,
        lead_first,
        inner_first,
        conv_first,
        head_first,
        gate_first,
        outer_first,
        lead_second,
        inner_second,
        conv_second,
        head_second,
        gate_second,
        outer_second,
    ):
        me = lax.axis_index("zero")
        rep = lax.axis_index("rep")
        core = rep & 1
        floor = rep >> 1

        def swap(value):
            return lax.ppermute(value, "rep", [(r, r ^ 1) for r in range(replicas)])

        def across(value, k):
            return lax.ppermute(value, "zero", [(i, i ^ k) for i in range(owners)])

        def up(value, k):
            return lax.ppermute(value, "rep", [(r, (((r >> 1) ^ k) << 1) | (r & 1)) for r in range(replicas)])

        def fetch(own):
            half = own.shape[0] // 2
            mine = lax.dynamic_slice_in_dim(own, core * half, half, 0)
            got = [across(mine, k) for k in range(1, owners)]
            return [own] + got + [swap(g) for g in got]

        def offsets(rows):
            half = rows // 2
            near = [(me ^ k) * rows + core * half for k in range(1, owners)]
            far = [(me ^ k) * rows + (1 - core) * half for k in range(1, owners)]
            return jnp.stack([me * rows] + near + far).astype(jnp.int32)

        def reduce_grad(send, keep):
            got = swap(send)
            parts = [
                (pick_at(keep, me ^ k).astype(f32) + pick_at(got, me ^ k).astype(f32)).astype(bf16)
                for k in range(owners)
            ]
            came = [across(parts[k], k) for k in range(1, owners)]
            total = tree_sum([v.astype(f32) for v in [parts[0]] + came]).astype(bf16)
            half, width = total.shape
            layers = total.reshape(depth, half // depth, width)
            parts = [pick_at(layers, floor ^ k) for k in range(depth)]
            came = [up(parts[k], k) for k in range(1, depth)]
            mine = tree_sum([v.astype(f32) for v in [parts[0]] + came]).astype(bf16)
            layers = lax.dynamic_update_index_in_dim(layers, mine, floor, 0)
            for k in range(1, depth):
                layers = lax.dynamic_update_index_in_dim(layers, up(mine, k), floor ^ k, 0)
            near = layers.reshape(half, width)
            far = swap(near)
            first = jnp.where(core == 0, near, far)
            second = jnp.where(core == 0, far, near)
            return jnp.concatenate([first, second], axis=0).astype(f32)

        def reduce_small(value):
            value = value.astype(bf16)
            value = (value.astype(f32) + swap(value).astype(f32)).astype(bf16)
            parts = [pick_at(value, me ^ k) for k in range(owners)]
            came = [across(parts[k], k) for k in range(1, owners)]
            total = tree_sum([v.astype(f32) for v in [parts[0]] + came]).astype(bf16)
            came = [up(total, k) for k in range(1, depth)]
            return tree_sum([v.astype(f32) for v in [total] + came])

        width_of = [v.size for v in (lead_gain, gate_gain, conv_table, head_table)]
        taken = sum(width_of)
        packed_rows = -(-taken // 2048) * 16

        def pack(values, lead_shape=()):
            flat = [v.reshape(lead_shape + (-1,)) for v in values]
            joined = jnp.concatenate(flat, axis=-1)
            fill = packed_rows * 128 - joined.shape[-1]
            joined = jnp.pad(joined, [(0, 0)] * len(lead_shape) + [(0, fill)])
            return joined.reshape(lead_shape + (packed_rows, 128))

        def unpack(value):
            flat = value.reshape(value.shape[:-2] + (-1,))
            at, out = 0, []
            for w in width_of:
                out.append(flat[..., at : at + w])
                at += w
            return out

        small = pack([v.astype(bf16) for v in (lead_gain, gate_gain, conv_table, head_table)])
        came = [small] + [across(small, k) for k in range(1, owners)]
        ordered = []
        for j in range(owners):
            value = came[0]
            for k in range(1, owners):
                value = jnp.where((me ^ k) == j, came[k], value)
            ordered.append(value)
        small_all = jnp.stack(ordered).astype(f32)
        lead_all, gate_all, conv_all, head_all = unpack(small_all)
        lead_low = lead_all.reshape(-1)
        gate_low = gate_all.reshape(-1)
        conv_low = conv_all.reshape(owners, K + 1, -1).transpose(1, 0, 2).reshape(K + 1, CONV)
        head_low = head_all.reshape(owners, 3, -1).transpose(1, 0, 2).reshape(3, H)

        mixed_shard = inner_weight[:, DI:].astype(bf16)
        gate_shard = inner_weight[:, :DI].astype(bf16)
        outer_shard = outer_weight.astype(bf16)
        in_parts = fetch(mixed_shard)
        out_parts = fetch(outer_shard)
        gate_parts = fetch(gate_shard)

        row_count, width = tokens.shape
        inner_rows = width // owners
        outer_rows = DI // owners
        ids = segment_ids
        rows = [ids.astype(f32)]
        for j in range(1, K):
            same = (ids[:-j] == ids[j:]).astype(f32)
            rows.append(jnp.concatenate([jnp.zeros((j,), f32), same]))
        for j in range(1, K):
            same = (ids[:-j] == ids[j:]).astype(f32)
            rows.append(jnp.concatenate([same, jnp.zeros((j,), f32)]))
        rows.append(jnp.zeros((LEN,), f32))
        rows = jnp.stack(rows).reshape(8, CH, Q).transpose(1, 0, 2)

        def rows8(value, cols):
            return jnp.pad(value, ((0, 8 - value.shape[0]), (0, cols - value.shape[1])))

        taps = rows8(conv_low, CONV)
        head = rows8(jnp.stack([head_low[0], -jnp.exp(head_low[1])]), 128)
        dskip = rows8(jnp.repeat(head_low[2], DI // H)[None], DI)
        gain = rows8(gate_low[None], DI)

        inputs = tokens.astype(f32)
        r1 = lax.rsqrt(jnp.mean(inputs * inputs, axis=-1, keepdims=True) + norm_eps)
        normed = (inputs * r1 * lead_low).astype(bf16)
        halves = normed.reshape(row_count, owners, 2, inner_rows // 2)
        turn_send = pick_at(halves, 1 - core, 2).reshape(row_count, -1).T
        turn_keep = pick_at(halves, core, 2).reshape(row_count, -1).T

        conv_in, step_in, in_full = project("project_in", offsets(inner_rows), normed, in_parts, owners, tail=H)
        y, acts, dsilu, states = scan_forward(ids, rows, conv_in, step_in, taps, head, dskip)
        gn_grad, outer_full = project("project_out_grad", offsets(outer_rows), cotangent, out_parts, owners, transposed=True)
        z, gate_full = project("project_gate", offsets(inner_rows), normed, gate_parts, owners)
        low, y_grad, z_grad, gate_sum = gate(y, z, gn_grad, gain)
        mixed = (inputs + dot(low, outer_full)).astype(bf16)

        low_halves = low.reshape(row_count, owners, 2, outer_rows // 2)

        def outer_part(which):
            part = pick_at(low_halves, which, 2)
            return jnp.einsum("tjr,te->jre", part, cotangent, preferred_element_type=f32).astype(bf16)

        outer_sum = reduce_grad(outer_part(1 - core), outer_part(core))

        def inner_part(turned, grad):
            return dot(turned, grad).astype(bf16).reshape(owners, inner_rows // 2, grad.shape[1])

        gate_in_sum = reduce_grad(inner_part(turn_send, z_grad), inner_part(turn_keep, z_grad))
        mix_grad, conv_sum, head_sum, skip_sum = scan_backward(
            ids, rows, acts, dsilu, conv_in, step_in, taps, head, dskip, states, y_grad, y
        )
        mix_in_sum = reduce_grad(inner_part(turn_send, mix_grad), inner_part(turn_keep, mix_grad))
        normed_grad = dot_nt(z_grad, gate_full) + dot_nt(mix_grad, in_full)
        q1 = normed_grad * lead_low
        back = r1 * (q1 - inputs * (r1 * r1 * jnp.mean(q1 * inputs, axis=-1, keepdims=True)))
        tokens_grad = (cotangent.astype(f32) + back).astype(bf16)
        lead_sum = jnp.sum(normed_grad * inputs * r1, axis=0)

        head_rows = jnp.concatenate([head_sum[:2, :H], skip_sum[0].reshape(1, H, DI // H).sum(-1)])

        def by_owner(value):
            return value.reshape(value.shape[0], owners, -1).transpose(1, 0, 2).reshape(owners, -1)

        small_sum = reduce_small(
            pack(
                [
                    lead_sum.reshape(owners, -1),
                    gate_sum[0].reshape(owners, -1),
                    by_owner(conv_sum[: K + 1]),
                    by_owner(head_rows),
                ],
                (owners,),
            )
        )
        lead_own, gate_own, conv_own, head_own = unpack(small_sum)
        conv_own = conv_own.reshape(conv_table.shape)
        head_own = head_own.reshape(head_table.shape)
        inner_own = jnp.concatenate([gate_in_sum, mix_in_sum], axis=1)

        sums = (lead_own, inner_own, conv_own, head_own, gate_own, outer_sum)
        weights = (lead_gain, inner_weight, conv_table, head_table, gate_gain, outer_weight)
        firsts = (lead_first, inner_first, conv_first, head_first, gate_first, outer_first)
        seconds = (lead_second, inner_second, conv_second, head_second, gate_second, outer_second)
        ups = [adam(*item) for item in zip(weights, sums, firsts, seconds)]
        return (
            (mixed, tokens_grad)
            + sums
            + tuple(up[0] for up in ups)
            + tuple(up[1] for up in ups)
            + tuple(up[2] for up in ups)
        )

    return body


def solution(mesh):
    flat, tall, wide = P("zero"), P("zero", None), P(None, "zero")
    group = (flat, tall, wide, wide, flat, tall)
    rows = P(("rep", "zero"), None)
    return jax.shard_map(
        make_body(mesh.shape["rep"], mesh.shape["zero"]),
        mesh=mesh,
        in_specs=(rows, P(("rep", "zero")), rows) + group * 3,
        out_specs=(rows, rows) + group * 4,
        check_vma=False,
    )
```
